32 devices in a mesh: parts: 2 (over x), tile: 16 (over z, y, core).
Axes of the slice: x: 2, y: 2, z: 4, core: 2. Of those that a mesh axis runs over, the one named last changes fastest.
Arguments:
- sections: bfloat16 [4096, 2048], P(('parts', 'tile')), parts along dimension 0, may hold values from -10 to 10
- valid_mask: int32 [32, 16], P(('parts', 'tile')), parts along dimension 0, may hold values 0 or 1
- coarse_offsets: int32 [8, 2], P('parts'), parts along dimension 0, may hold values from -3 to 3
Outputs:
- aligned: bfloat16 [4096, 2048], P(('parts', 'tile')), parts along dimension 0
- node_shift: float32 [2, 32, 16], P(None, ('parts', 'tile')), parts along dimension 1
The draws below stay inside these ranges and needn't reach their ends.
There are 2 independent parts, one for each index of `parts`. The reference program is written for one: setup_inputs(seed, part) draws one part's arguments, and reference() takes and returns one part's arrays. A program takes and returns all parts, laid end to end along the dimension named above; each array names one. Nothing has to cross between parts.
All inputs are finite; a program needn't handle non-finite values. No bound on the sum of `valid_mask` on one device may be relied on, other than what follows from the above.
Results may differ from the reference program's by a relative error of at most 0.002.
Values may be sent and summed in bfloat16 or wider, within the bound.
A program may use at most 64 MiB of HBM per device.

```python
import jax
import jax.numpy as jnp
from jax import lax

SECTIONS = 4
PATCH = 128
PC = 16
HALF = 4
SWEEPS = 3
TPS = 4


def draw_sections(key, part):
    row_count = TPS * PATCH
    col_count = PC * PATCH
    common_key = jax.random.fold_in(key, 11)
    own_key = jax.random.fold_in(key, 12)
    common = jax.random.normal(common_key, (row_count, col_count), jnp.float32)
    own_part = jax.random.normal(own_key, (SECTIONS, row_count, col_count), jnp.float32)
    volume = jnp.clip(0.6 * common[None] + 0.8 * own_part, -6.0, 6.0)
    return volume.reshape(SECTIONS * row_count, col_count).astype(jnp.bfloat16)


def touch_ends(drawn, stream_key, least, largest):
    spot = [jax.random.randint(jax.random.fold_in(stream_key, axis), (), 0, length) for axis, length in enumerate(drawn.shape)]
    widest = drawn.shape.index(max(drawn.shape))
    neighbour = spot[:widest] + [(spot[widest] + 1) % drawn.shape[widest]] + spot[widest + 1:]
    return drawn.at[tuple(spot)].set(least).at[tuple(neighbour)].set(largest)


def setup_inputs(seed: int = 0, part: int = 0) -> dict:
    splits = jax.random.split(jax.random.key(seed), 4)
    part_keys = jax.random.split(jax.random.fold_in(splits[3], part), 4)
    sections = draw_sections(jax.random.fold_in(jax.random.fold_in(splits[3], part), 71), part)
    valid_mask = touch_ends((jax.random.randint(part_keys[1], (SECTIONS * TPS, PC), 0, 4) < 3).astype(jnp.int32), jax.random.fold_in(part_keys[1], 1), 0, 1)
    coarse_offsets = touch_ends(jax.random.randint(part_keys[2], (SECTIONS, 2), -3, 4), jax.random.fold_in(part_keys[2], 1), -3, 3).astype(jnp.int32)
    return {"sections": sections, "valid_mask": valid_mask, "coarse_offsets": coarse_offsets}


highest = lax.Precision.HIGHEST
sharpness = 12.0
anchor_weight = 2.0

def fourier_tables(length):
    index_vector = jnp.arange(length, dtype=jnp.int32)
    phase_index = index_vector[:, None] * index_vector[None, :] % length
    angles = phase_index.astype(jnp.float32) * (2.0 * jnp.pi / length)
    return (jnp.cos(angles), -jnp.sin(angles))

def left_apply(matrix, blocks):
    return jnp.einsum('jk,...kl->...jl', matrix, blocks, precision=highest)

def right_apply(blocks, matrix):
    return jnp.einsum('...jk,kl->...jl', blocks, matrix, precision=highest)

def forward(blocks, cosine_table, sine_table):
    first_re = left_apply(cosine_table, blocks)
    first_im = left_apply(sine_table, blocks)
    out_re = right_apply(first_re, cosine_table) - right_apply(first_im, sine_table)
    out_im = right_apply(first_re, sine_table) + right_apply(first_im, cosine_table)
    return (out_re, out_im)

def centred(blocks):
    mean_level = lax.optimization_barrier(jnp.mean(blocks, axis=(-2, -1), keepdims=True))
    centre = blocks - mean_level
    spread = jnp.sqrt(lax.optimization_barrier(jnp.mean(centre * centre, axis=(-2, -1), keepdims=True)) + 1e-05)
    return (centre, mean_level, spread)

def window_tables(offset, length):
    shift_values = offset + jnp.arange(-HALF, HALF + 1, dtype=jnp.int32)
    frequency = jnp.arange(length, dtype=jnp.int32)
    phase_index = jnp.mod(shift_values[:, None] * frequency[None, :], length)
    angles = phase_index.astype(jnp.float32) * (2.0 * jnp.pi / length)
    return (jnp.cos(angles), jnp.sin(angles), shift_values.astype(jnp.float32))

def estimate_flow(own_re, own_im, own_spread, prev_re, prev_im, prev_spread, offset_pair):
    length = PATCH
    cross_re = own_re * prev_re + own_im * prev_im
    cross_im = own_im * prev_re - own_re * prev_im
    row_cos, row_sin, row_shifts = window_tables(offset_pair[0], length)
    col_cos, col_sin, col_shifts = window_tables(offset_pair[1], length)
    half_re = left_apply(row_cos, cross_re) - left_apply(row_sin, cross_im)
    half_im = left_apply(row_cos, cross_im) + left_apply(row_sin, cross_re)
    correlation = jnp.einsum('...jk,lk->...jl', half_re, col_cos, precision=highest) - jnp.einsum('...jk,lk->...jl', half_im, col_sin, precision=highest)
    similarity = correlation / (float(length) ** 4 * own_spread * prev_spread)
    weights = jnp.exp(sharpness * similarity)
    weight_sum = lax.optimization_barrier(jnp.sum(weights, axis=(-2, -1), keepdims=True))
    chance = weights / weight_sum
    flow_rows = lax.optimization_barrier(jnp.sum(chance * row_shifts[:, None], axis=(-2, -1)))
    flow_cols = lax.optimization_barrier(jnp.sum(chance * col_shifts[None, :], axis=(-2, -1)))
    return jnp.stack([flow_rows, flow_cols], axis=0)

def warp_patches(spec_re, spec_im, mean_level, shift_rows, shift_cols, cosine_table, sine_table):
    length = PATCH
    frequency = jnp.arange(length, dtype=jnp.int32)
    signed_freq = jnp.where(frequency < length // 2, frequency, frequency - length).astype(jnp.float32)
    phase_angle = 2.0 * jnp.pi / length * (signed_freq[:, None] * shift_rows[..., None, None] + signed_freq[None, :] * shift_cols[..., None, None])
    turn_cos = jnp.cos(phase_angle)
    turn_sin = jnp.sin(phase_angle)
    moved_re = spec_re * turn_cos - spec_im * turn_sin
    moved_im = spec_re * turn_sin + spec_im * turn_cos
    back_re = cosine_table
    back_im = -sine_table
    inner_re = left_apply(back_re, moved_re) - left_apply(back_im, moved_im)
    inner_im = left_apply(back_re, moved_im) + left_apply(back_im, moved_re)
    restored = right_apply(inner_re, back_re) - right_apply(inner_im, back_im)
    return restored / float(length * length) + mean_level

def relax_mesh(flow_nodes, mask_float):
    weight = anchor_weight * mask_float
    padded_ones = jnp.pad(jnp.ones_like(mask_float), 1)
    neighbour_count = padded_ones[:-2, 1:-1] + padded_ones[2:, 1:-1] + padded_ones[1:-1, :-2] + padded_ones[1:-1, 2:]
    node_shift = flow_nodes * mask_float
    for sweep_index in range(SWEEPS):
        padded = jnp.pad(node_shift, ((0, 0), (1, 1), (1, 1)))
        neighbours = padded[:, :-2, 1:-1] + padded[:, 2:, 1:-1] + padded[:, 1:-1, :-2] + padded[:, 1:-1, 2:]
        node_shift = (weight * flow_nodes + neighbours) / (weight + neighbour_count)
    return node_shift

def to_patches(strip):
    return strip.astype(jnp.float32).reshape(-1, PATCH, PC, PATCH).transpose(0, 2, 1, 3)

def from_patches(patches):
    return patches.transpose(0, 2, 1, 3).reshape(-1, PC * PATCH)

def reference(sections, valid_mask, coarse_offsets):
    half_rows = TPS // 2
    sections = jnp.roll(sections, -half_rows * PATCH, axis=0)
    valid_mask = jnp.roll(valid_mask, -half_rows, axis=0)
    cosine_table, sine_table = fourier_tables(PATCH)
    strip_rows = TPS * PATCH
    aligned_list = [sections[:strip_rows]]
    shift_list = [jnp.zeros((2, TPS, PC), jnp.float32)]
    previous = sections[:strip_rows]
    for section_index in range(1, SECTIONS):
        current = to_patches(sections[section_index * strip_rows:(section_index + 1) * strip_rows])
        own_centre, own_level, own_spread = centred(current)
        own_re, own_im = forward(own_centre, cosine_table, sine_table)
        prev_patches = to_patches(lax.optimization_barrier(previous))
        prev_centre, prev_level, prev_spread = centred(prev_patches)
        prev_re, prev_im = forward(prev_centre, cosine_table, sine_table)
        flow_nodes = estimate_flow(own_re, own_im, own_spread, prev_re, prev_im, prev_spread, coarse_offsets[section_index])
        mask_float = valid_mask[section_index * TPS:(section_index + 1) * TPS].astype(jnp.float32)
        node_shift = relax_mesh(flow_nodes, mask_float)
        warped = warp_patches(own_re, own_im, own_level, node_shift[0], node_shift[1], cosine_table, sine_table).astype(jnp.bfloat16)
        strip = from_patches(warped)
        previous = strip
        aligned_list.append(strip)
        shift_list.append(node_shift)
    aligned_all = jnp.roll(jnp.concatenate(aligned_list, axis=0), half_rows * PATCH, axis=0)
    shift_all = jnp.roll(jnp.concatenate(shift_list, axis=1), half_rows, axis=1)
    return (aligned_all, shift_all)
```

```python
import functools

import jax
import jax.numpy as jnp
import numpy as np
from jax import lax
from jax.experimental import pallas as pl
from jax.experimental.pallas import tpu as pltpu
from jax.sharding import PartitionSpec as P

SECTIONS = 4
PATCH = 128
HALF = 4
SWEEPS = 3
REACH = 3
WINDOW = 2 * HALF + 1
PADDED = 16
LANES = 128

sharpness = 12.0
anchor_weight = 2.0
MESH = pl.DeviceIdType.MESH
f32 = jnp.float32
bf16 = jnp.bfloat16


def split(value):
    high = value.astype(bf16)
    return high, (value - high.astype(f32)).astype(bf16)


def mm(a, b):
    return jnp.dot(a, b, preferred_element_type=f32)


def mm_nt(a, b):
    return lax.dot_general(a, b, (((1,), (1,)), ((), ())), preferred_element_type=f32)


def mm3(a, b, product=mm):
    return product(a[0], b[0]) + (product(a[0], b[1]) + product(a[1], b[0]))


def np_split(value):
    value = np.asarray(value, np.float32)
    high = np.asarray(value, bf16)
    low = np.asarray(value - high.astype(np.float32), bf16)
    return high, low


def constants():
    n = PATCH
    k = np.arange(n)
    angle = 2 * np.pi * ((k[:, None] * k[None, :]) % n) / n
    stacked = np.concatenate([np.cos(angle), np.sin(angle)], axis=0)
    dft_hi, dft_lo = np_split(stacked)
    dft_t_hi, dft_t_lo = np_split(stacked.T)
    u = np.arange(-HALF - REACH, -HALF - REACH + 24)
    window_angle = 2 * np.pi * ((u[:, None] * k[None, :]) % n) / n
    window = np.stack([np.cos(window_angle), np.sin(window_angle)]).astype(np.float32)
    gap = k[:, None] - k[None, :]
    half_angle = np.pi * gap / n
    warp = np.stack(
        [
            np.sin(half_angle),
            np.cos(half_angle),
            (1.0 - 2.0 * (gap % 2)) * np.ones((n, n)),
            gap % n,
        ]
    ).astype(np.float32)
    return dft_hi, dft_lo, dft_t_hi, dft_t_lo, window, warp


def shift_terms(d):
    whole = jnp.round(d)
    frac = d - whole
    odd = jnp.abs(whole - 2.0 * jnp.round(whole * 0.5))
    sine = jnp.sin(jnp.pi * frac)
    signed = jnp.where(odd > 0.5, -sine, sine) * (1.0 / PATCH)
    angle = d * (np.pi / PATCH)
    tangent = jnp.sin(angle) / jnp.cos(angle)
    small = frac * (np.pi / PATCH)
    tiny = jnp.abs(frac) < 1e-6
    peak = jnp.where(
        tiny, 1.0, sine * jnp.cos(small) / jnp.where(tiny, 1.0, PATCH * jnp.sin(small))
    )
    return tangent, signed, peak, whole


def interpolation(terms, tables, transposed):
    tangent, signed, peak, whole = terms
    sine, cosine, parity, gap = tables
    if transposed:
        bottom = cosine * tangent - sine
        top = cosine + sine * tangent
        centre = jnp.where(whole < 0, whole + PATCH, whole)
    else:
        bottom = cosine * tangent + sine
        top = cosine - sine * tangent
        centre = jnp.where(whole > 0, PATCH - whole, -whole)
    value = jnp.where(gap == centre, peak, (signed * parity) * (top / bottom))
    return split(value)


def warp_patch(patch, column, checker, tables):
    row_terms = [column[i : i + 1, :] for i in range(4)]
    col_terms = [column[i : i + 1, :] for i in range(4, 8)]
    right = interpolation(col_terms, tables, True)
    left = interpolation(row_terms, tables, False)
    inner = split(mm(patch, right[0]) + mm(patch, right[1]))
    corner = row_terms[1] * col_terms[1] * checker
    return mm3(left, inner) - corner * tables[2]


def total(value):
    return jnp.sum(jnp.sum(value, axis=0, keepdims=True), axis=1, keepdims=True)


def term_rows(d_rows, d_cols):
    both = jnp.concatenate([d_rows, d_cols], axis=0)
    tangent, signed, peak, whole = shift_terms(both)
    pieces = [t[i : i + 1] for i in range(2) for t in (tangent, signed, peak, whole)]
    return jnp.concatenate(pieces, axis=0)


def centred(patch):
    mean_level = total(patch) * (1.0 / (PATCH * PATCH))
    centre = patch - mean_level
    variance = total(centre * centre) * (1.0 / (PATCH * PATCH))
    return centre, jnp.sqrt(variance + 1e-05)


def patch_slices(width):
    return [slice(i * PATCH, (i + 1) * PATCH) for i in range(width // PATCH)]


def chain_kernel(
    tile_count,
    grid_cols,
    offsets,
    mask_ref,
    dft_hi,
    dft_lo,
    dft_t_hi,
    dft_t_lo,
    window,
    warp_tables,
    strip,
    out_ref,
    raw,
    mask_tile,
    mask_slots,
    flow_tile,
    flow_slots,
    spec_re,
    spec_im,
    local_sem,
    strip_send,
    strip_recv,
    mask_send,
    mask_recv,
    flow_send,
    flow_recv,
):
    per_section = tile_count // SECTIONS
    me = lax.axis_index("tile")
    lead = per_section // 2
    rotated = lax.rem(me + tile_count - lead, tile_count)
    group = rotated // per_section
    row = lax.rem(rotated, per_section)
    quarter = raw.shape[2]
    quarter_nodes = quarter // PATCH
    slices = patch_slices(quarter)

    barrier = pltpu.get_barrier_semaphore()
    for step in range(1, tile_count):
        peer = lax.rem(me + step, tile_count)
        pl.semaphore_signal(barrier, inc=1, device_id={"tile": peer}, device_id_type=MESH)

    own = pltpu.make_async_copy(
        strip.at[:, pl.ds(pl.multiple_of(group * quarter, LANES), quarter)],
        raw.at[group],
        local_sem,
    )
    own.start()
    shape = (2 * per_section, LANES)
    sub = lax.broadcasted_iota(jnp.int32, shape, 0)
    lane = lax.broadcasted_iota(jnp.int32, shape, 1)
    sub_row = lax.rem(sub, per_section)
    mask_tile[...] = jnp.zeros(shape, f32)
    mask_tile[0:1, 0:grid_cols] = mask_ref[...].astype(f32)
    mask_row = mask_tile[0:1, :]
    mask_tile[...] = jnp.where(sub_row == row, mask_row, 0.0)
    mask_slots[me] = mask_tile[...]

    pl.semaphore_wait(barrier, tile_count - 1)

    sends = []
    for step in range(1, SECTIONS):
        target_group = lax.rem(group + step, SECTIONS)
        target = lax.rem(me + step * per_section, tile_count)
        copy = pltpu.make_async_remote_copy(
            src_ref=strip.at[
                :, pl.ds(pl.multiple_of(target_group * quarter, LANES), quarter)
            ],
            dst_ref=raw.at[group],
            send_sem=strip_send.at[step],
            recv_sem=strip_recv.at[step],
            device_id={"tile": target},
            device_id_type=MESH,
        )
        copy.start()
        sends.append(copy)
    mask_copies = []
    for step in range(1, tile_count):
        peer = lax.rem(me + step, tile_count)
        copy = pltpu.make_async_remote_copy(
            src_ref=mask_tile,
            dst_ref=mask_slots.at[me],
            send_sem=mask_send.at[step],
            recv_sem=mask_recv.at[step],
            device_id={"tile": peer},
            device_id_type=MESH,
        )
        copy.start()
        mask_copies.append(copy)

    tables = [warp_tables[i] for i in range(4)]
    dft = (dft_hi[...], dft_lo[...])
    dft_t = (dft_t_hi[...], dft_t_lo[...])

    def spectra(centres):
        strip0 = jnp.concatenate(centres, axis=1)
        first = split(mm3(dft, split(strip0)))
        found = []
        for s in slices:
            both = mm3((first[0][:, s], first[1][:, s]), dft_t)
            real = both[:PATCH, :PATCH] - both[PATCH:, PATCH:]
            imag = -(both[:PATCH, PATCH:] + both[PATCH:, :PATCH])
            found.append((real, imag))
        return found

    def own_spectra(section):
        pieces = [centred(raw[section, :, s].astype(f32)) for s in slices]
        found = spectra([piece[0] for piece in pieces])
        for i, (real, imag) in enumerate(found):
            spec_re[i] = real
            spec_im[i] = imag
        return [piece[1] for piece in pieces]

    up_ok = (sub_row > 0).astype(f32)
    down_ok = (sub_row < per_section - 1).astype(f32)
    left_ok = jnp.logical_and(lane > 0, lane < grid_cols).astype(f32)
    right_ok = (lane < grid_cols - 1).astype(f32)
    count = up_ok + down_ok + left_ok + right_ok

    def relax(flow, mask):
        weight = anchor_weight * mask
        pull = weight * flow
        scale = 1.0 / (weight + count)
        d = flow * mask
        for _ in range(SWEEPS):
            near = (
                up_ok * pltpu.roll(d, 1, 0)
                + down_ok * pltpu.roll(d, 2 * per_section - 1, 0)
                + left_ok * pltpu.roll(d, 1, 1)
                + right_ok * pltpu.roll(d, LANES - 1, 1)
            )
            d = (pull + near) * scale
        return jnp.where(lane < grid_cols, d, 0.0)

    corr_row = lax.broadcasted_iota(jnp.int32, (PADDED, PADDED), 0)
    corr_col = lax.broadcasted_iota(jnp.int32, (PADDED, PADDED), 1)
    inside = jnp.logical_and(corr_row < WINDOW, corr_col < WINDOW)
    home = jnp.zeros(shape, f32)

    own.wait()
    for copy in sends:
        copy.wait()

    own_spread = own_spectra(1)
    d = None
    for section in range(1, SECTIONS):
        if section == 1:
            previous = [raw[0, :, s].astype(f32) for s in slices]
        else:
            pick_rows = jnp.sum(
                jnp.where(sub == row, d, 0.0), axis=0, keepdims=True
            )
            pick_cols = jnp.sum(
                jnp.where(sub == row + per_section, d, 0.0), axis=0, keepdims=True
            )
            terms = term_rows(pick_rows, pick_cols)
            term_lane = lax.broadcasted_iota(jnp.int32, terms.shape, 1)
            previous = []
            for i, s in enumerate(slices):
                wanted = term_lane == group * quarter_nodes + i
                column = jnp.sum(jnp.where(wanted, terms, 0.0), axis=1, keepdims=True)
                patch = raw[section - 1, :, s]
                checker = total(patch.astype(f32) * tables[2])
                moved = warp_patch(patch, column, checker, tables)
                previous.append(moved.astype(bf16).astype(f32))
        pieces = [centred(patch) for patch in previous]
        found = spectra([piece[0] for piece in pieces])
        row_offset = offsets[section, 0]
        col_offset = offsets[section, 1]
        row_cos = window[0, pl.ds(row_offset + REACH, PADDED), :]
        row_sin = window[1, pl.ds(row_offset + REACH, PADDED), :]
        col_cos = split(window[0, pl.ds(col_offset + REACH, PADDED), :])
        col_sin = split(window[1, pl.ds(col_offset + REACH, PADDED), :])
        row_table = split(jnp.concatenate([row_cos, row_sin], axis=0))
        row_shift = (corr_row - HALF + row_offset).astype(f32)
        col_shift = (corr_col - HALF + col_offset).astype(f32)
        half_re, half_im = [], []
        for i, (prev_re, prev_im) in enumerate(found):
            own_re, own_im = spec_re[i], spec_im[i]
            cross_re = own_re * prev_re + own_im * prev_im
            cross_im = own_im * prev_re - own_re * prev_im
            part_re = mm3(row_table, split(cross_re))
            part_im = mm3(row_table, split(cross_im))
            half_re.append(part_re[:PADDED] - part_im[PADDED:])
            half_im.append(part_im[:PADDED] + part_re[PADDED:])
        correlation = mm3(
            split(jnp.concatenate(half_re, axis=0)), col_cos, mm_nt
        ) - mm3(split(jnp.concatenate(half_im, axis=0)), col_sin, mm_nt)
        tile = jnp.zeros(shape, f32)
        for i in range(quarter_nodes):
            scale = sharpness / (float(PATCH) ** 4 * own_spread[i] * pieces[i][1])
            score = correlation[i * PADDED : (i + 1) * PADDED] * scale
            weights = jnp.where(inside, jnp.exp(score), 0.0)
            inverse = 1.0 / total(weights)
            flow_row = total(weights * row_shift) * inverse
            flow_col = total(weights * col_shift) * inverse
            here = lane == group * quarter_nodes + i
            tile = tile + jnp.where(
                jnp.logical_and(here, sub == row), flow_row, 0.0
            )
            tile = tile + jnp.where(
                jnp.logical_and(here, sub == row + per_section), flow_col, 0.0
            )
        index = section - 1
        flow_tile[index] = tile
        copies = []
        for step in range(1, tile_count):
            peer = lax.rem(me + step, tile_count)
            copy = pltpu.make_async_remote_copy(
                src_ref=flow_tile.at[index],
                dst_ref=flow_slots.at[index, step],
                send_sem=flow_send.at[index, step],
                recv_sem=flow_recv.at[index, step],
                device_id={"tile": peer},
                device_id_type=MESH,
            )
            copy.start()
            copies.append(copy)
        if section < SECTIONS - 1:
            own_spread = own_spectra(section + 1)
        if section == 1:
            for copy in mask_copies:
                copy.wait()
        mask = jnp.zeros(shape, f32)
        for r in range(per_section):
            mask = mask + mask_slots[(section * per_section + r + lead) % tile_count]
        for copy in copies:
            copy.wait()
        flow = tile
        for step in range(1, tile_count):
            flow = flow + flow_slots[index, step]
        d = relax(flow, mask)
        home = jnp.where(group == section, d, home)
    out_row = jnp.sum(jnp.where(sub == row, home, 0.0), axis=0, keepdims=True)
    out_col = jnp.sum(jnp.where(sub == row + per_section, home, 0.0), axis=0, keepdims=True)
    out_ref[...] = jnp.concatenate([out_row, out_col], axis=0)


def warp_kernel(shift_ref, strip, warp_tables, out_ref, node_ref):
    tables = [warp_tables[i] for i in range(4)]
    terms = term_rows(shift_ref[0:1, :], shift_ref[1:2, :])
    lane = lax.broadcasted_iota(jnp.int32, terms.shape, 1)
    nodes = node_ref.shape[2]
    node_ref[0] = shift_ref[0:1, 0:nodes]
    node_ref[1] = shift_ref[1:2, 0:nodes]
    for i, s in enumerate(patch_slices(strip.shape[1])):
        column = jnp.sum(jnp.where(lane == i, terms, 0.0), axis=1, keepdims=True)
        patch = strip[:, s]
        checker = total(patch.astype(f32) * tables[2])
        out_ref[:, s] = warp_patch(patch, column, checker, tables).astype(bf16)


def shards(tile_count, sections, valid_mask, coarse_offsets):
    dft_hi, dft_lo, dft_t_hi, dft_t_lo, window, warp = constants()
    per_section = tile_count // SECTIONS
    grid_cols = valid_mask.shape[1]
    quarter = sections.shape[1] // SECTIONS
    nodes = quarter // PATCH
    steps = SECTIONS - 1
    tile_shape = (2 * per_section, LANES)
    vmem = pl.BlockSpec(memory_space=pltpu.VMEM)
    shift = pl.pallas_call(
        functools.partial(chain_kernel, tile_count, grid_cols),
        out_shape=jax.ShapeDtypeStruct((2, LANES), f32),
        in_specs=[pl.BlockSpec(memory_space=pltpu.SMEM)]
        + [vmem] * 7
        + [pl.BlockSpec(memory_space=pl.ANY)],
        out_specs=vmem,
        scratch_shapes=[
            pltpu.VMEM((SECTIONS, PATCH, quarter), bf16),
            pltpu.VMEM(tile_shape, f32),
            pltpu.VMEM((tile_count,) + tile_shape, f32),
            pltpu.VMEM((steps,) + tile_shape, f32),
            pltpu.VMEM((steps, tile_count) + tile_shape, f32),
            pltpu.VMEM((nodes, PATCH, PATCH), f32),
            pltpu.VMEM((nodes, PATCH, PATCH), f32),
            pltpu.SemaphoreType.DMA,
            pltpu.SemaphoreType.DMA((SECTIONS,)),
            pltpu.SemaphoreType.DMA((SECTIONS,)),
            pltpu.SemaphoreType.DMA((tile_count,)),
            pltpu.SemaphoreType.DMA((tile_count,)),
            pltpu.SemaphoreType.DMA((steps, tile_count)),
            pltpu.SemaphoreType.DMA((steps, tile_count)),
        ],
        compiler_params=pltpu.CompilerParams(
            collective_id=0, has_side_effects=True, vmem_limit_bytes=48 * 1024 * 1024
        ),
        name="chain",
    )(coarse_offsets, valid_mask, dft_hi, dft_lo, dft_t_hi, dft_t_lo, window, warp, sections)
    return pl.pallas_call(
        warp_kernel,
        out_shape=(
            jax.ShapeDtypeStruct(sections.shape, bf16),
            jax.ShapeDtypeStruct((2, 1, grid_cols), f32),
        ),
        in_specs=[vmem, vmem, vmem],
        out_specs=(vmem, vmem),
        name="warp",
    )(shift, sections, warp)


def solution(mesh):
    placed = (P(("parts", "tile"), None), P(("parts", "tile"), None), P("parts", None))
    return jax.shard_map(
        functools.partial(shards, mesh.shape["tile"]),
        mesh=mesh,
        in_specs=placed,
        out_specs=(P(("parts", "tile"), None), P(None, ("parts", "tile"), None)),
        check_vma=False,
    )
```

```python
import functools

import jax
import jax.numpy as jnp
import numpy as np
from jax import lax
from jax.experimental import pallas as pl
from jax.experimental.pallas import tpu as pltpu
from jax.sharding import PartitionSpec as P

SECTIONS = 4
PATCH = 128
HALF = 4
SWEEPS = 3
REACH = 3
WINDOW = 2 * HALF + 1
PADDED = 16
LANES = 128
CONSTANTS = 6
HALVES = 2
PIECES = 4

sharpness = 12.0
anchor_weight = 2.0
MESH = pl.DeviceIdType.MESH
f32 = jnp.float32
bf16 = jnp.bfloat16


def split(value):
    high = value.astype(bf16)
    return high, (value - high.astype(f32)).astype(bf16)


def mm(a, b):
    return jnp.dot(a, b, preferred_element_type=f32)


def mm_nt(a, b):
    return lax.dot_general(a, b, (((1,), (1,)), ((), ())), preferred_element_type=f32)


def mm3(a, b, product=mm):
    return product(a[0], b[0]) + (product(a[0], b[1]) + product(a[1], b[0]))


def np_split(value):
    value = np.asarray(value, np.float32)
    high = np.asarray(value, bf16)
    low = np.asarray(value - high.astype(np.float32), bf16)
    return high, low


def constants():
    n = PATCH
    k = np.arange(n)
    angle = 2 * np.pi * ((k[:, None] * k[None, :]) % n) / n
    stacked = np.concatenate([np.cos(angle), np.sin(angle)], axis=0)
    dft_hi, dft_lo = np_split(stacked)
    dft_t_hi, dft_t_lo = np_split(stacked.T)
    u = np.arange(-HALF - REACH, -HALF - REACH + 24)
    window_angle = 2 * np.pi * ((u[:, None] * k[None, :]) % n) / n
    window = np.stack([np.cos(window_angle), np.sin(window_angle)]).astype(np.float32)
    gap = k[:, None] - k[None, :]
    half_angle = np.pi * gap / n
    warp = np.stack(
        [
            np.sin(half_angle),
            np.cos(half_angle),
            (1.0 - 2.0 * (gap % 2)) * np.ones((n, n)),
            gap % n,
        ]
    ).astype(np.float32)
    return dft_hi, dft_lo, dft_t_hi, dft_t_lo, window, warp


def shift_terms(d):
    whole = jnp.round(d)
    frac = d - whole
    odd = jnp.abs(whole - 2.0 * jnp.round(whole * 0.5))
    sine = jnp.sin(jnp.pi * frac)
    signed = jnp.where(odd > 0.5, -sine, sine) * (1.0 / PATCH)
    angle = d * (np.pi / PATCH)
    tangent = jnp.sin(angle) / jnp.cos(angle)
    small = frac * (np.pi / PATCH)
    tiny = jnp.abs(frac) < 1e-6
    peak = jnp.where(
        tiny, 1.0, sine * jnp.cos(small) / jnp.where(tiny, 1.0, PATCH * jnp.sin(small))
    )
    return tangent, signed, peak, whole


def interpolation(terms, tables, transposed):
    tangent, signed, peak, whole = terms
    sine, cosine, parity, gap = tables
    if transposed:
        bottom = cosine * tangent - sine
        top = cosine + sine * tangent
        centre = jnp.where(whole < 0, whole + PATCH, whole)
    else:
        bottom = cosine * tangent + sine
        top = cosine - sine * tangent
        centre = jnp.where(whole > 0, PATCH - whole, -whole)
    value = jnp.where(gap == centre, peak, (signed * parity) * (top / bottom))
    return split(value)


def warp_patch(patch, column, checker, tables):
    row_terms = [column[i : i + 1, :] for i in range(4)]
    col_terms = [column[i : i + 1, :] for i in range(4, 8)]
    right = interpolation(col_terms, tables, True)
    left = interpolation(row_terms, tables, False)
    inner = split(mm(patch, right[0]) + mm(patch, right[1]))
    corner = row_terms[1] * col_terms[1] * checker
    return mm3(left, inner) - corner * tables[2]


def total(value):
    return jnp.sum(jnp.sum(value, axis=0, keepdims=True), axis=1, keepdims=True)


def term_rows(d_rows, d_cols):
    both = jnp.concatenate([d_rows, d_cols], axis=0)
    tangent, signed, peak, whole = shift_terms(both)
    pieces = [t[i : i + 1] for i in range(2) for t in (tangent, signed, peak, whole)]
    return jnp.concatenate(pieces, axis=0)


def centred(patch):
    mean_level = total(patch) * (1.0 / (PATCH * PATCH))
    centre = patch - mean_level
    variance = total(centre * centre) * (1.0 / (PATCH * PATCH))
    return centre, jnp.sqrt(variance + 1e-05)


def patch_slices(width):
    return [slice(i * PATCH, (i + 1) * PATCH) for i in range(width // PATCH)]


def chain_kernel(
    tile_count,
    grid_cols,
    offsets_in,
    mask_in,
    *rest,
):
    constant_in = rest[:CONSTANTS]
    constant_ref = rest[CONSTANTS + 2 : 2 * CONSTANTS + 2]
    (dft_hi, dft_lo, dft_t_hi, dft_t_lo, window, warp_tables) = constant_ref
    strip, out_ref = rest[CONSTANTS : CONSTANTS + 2]
    (
    offsets,
    mask_ref,
    load_sem,
    raw,
    mask_tile,
    mask_slots,
    flow_tile,
    flow_slots,
    flow_sum,
    spec_re,
    spec_im,
    strip_send,
    strip_recv,
    mask_send,
    mask_recv,
    flow_send,
    flow_recv,
    ) = rest[2 * CONSTANTS + 2 :]
    per_section = tile_count // SECTIONS
    me = lax.axis_index("tile")
    lead = per_section // 2
    rotated = lax.rem(me + tile_count - lead, tile_count)
    group = rotated // per_section
    row = lax.rem(rotated, per_section)
    chain = me // per_section
    quarter = raw.shape[3] * HALVES
    part = raw.shape[3]
    quarter_nodes = quarter // PATCH
    part_nodes = part // PATCH
    reach = -(-SWEEPS // quarter_nodes)

    barrier = pltpu.get_barrier_semaphore()
    for step in range(1, tile_count):
        peer = lax.rem(me + step, tile_count)
        pl.semaphore_signal(barrier, inc=1, device_id={"tile": peer}, device_id_type=MESH)

    loads = [
        pltpu.make_async_copy(source, target, load_sem.at[i])
        for i, (source, target) in enumerate(
            zip((mask_in, offsets_in) + constant_in, (mask_ref, offsets) + constant_ref)
        )
    ]
    for copy in loads:
        copy.start()
    def columns(owner, half):
        return strip.at[:, pl.ds(pl.multiple_of(owner * quarter + half * part, LANES), part)]

    for half in range(HALVES):
        pltpu.make_async_copy(
            columns(chain, half), raw.at[group, half], strip_recv.at[group, half]
        ).start()
    loads[0].wait()
    shape = (2 * per_section, LANES)
    sub = lax.broadcasted_iota(jnp.int32, shape, 0)
    lane = lax.broadcasted_iota(jnp.int32, shape, 1)
    sub_row = lax.rem(sub, per_section)
    mask_tile[...] = jnp.zeros(shape, f32)
    mask_tile[0:1, 0:grid_cols] = mask_ref[...].astype(f32)
    mask_row = mask_tile[0:1, :]
    mask_tile[...] = jnp.where(sub_row == row, mask_row, 0.0)
    mask_slots[me] = mask_tile[...]

    pl.semaphore_wait(barrier, tile_count - 1)

    mask_copies = []
    for step in range(1, tile_count):
        peer = lax.rem(me + step, tile_count)
        copy = pltpu.make_async_remote_copy(
            src_ref=mask_tile,
            dst_ref=mask_slots.at[me],
            send_sem=mask_send.at[step],
            recv_sem=mask_recv.at[step],
            device_id={"tile": peer},
            device_id_type=MESH,
        )
        copy.start()
        mask_copies.append(copy)

    sends = []
    for half in range(HALVES):
        for step in range(1, SECTIONS):
            copy = pltpu.make_async_remote_copy(
                src_ref=columns(lax.rem(chain + step, SECTIONS), half),
                dst_ref=raw.at[group, half],
                send_sem=strip_send.at[step, half],
                recv_sem=strip_recv.at[group, half],
                device_id={"tile": lax.rem(me + step * per_section, tile_count)},
                device_id_type=MESH,
            )
            copy.start()
            sends.append(copy)
    for copy in loads[1:]:
        copy.wait()
    tables = [warp_tables[i] for i in range(4)]
    dft = (dft_hi[...], dft_lo[...])
    dft_t = (dft_t_hi[...], dft_t_lo[...])

    def spectra(centres):
        strip0 = jnp.concatenate(centres, axis=1)
        first = split(mm3(dft, split(strip0)))
        found = []
        for s in patch_slices(strip0.shape[1]):
            both = mm3((first[0][:, s], first[1][:, s]), dft_t)
            real = both[:PATCH, :PATCH] - both[PATCH:, PATCH:]
            imag = -(both[:PATCH, PATCH:] + both[PATCH:, :PATCH])
            found.append((real, imag))
        return found

    def patch_of(section, i):
        start = (i % part_nodes) * PATCH
        return raw[section, i // part_nodes, :, start : start + PATCH]

    def own_spectra(section, nodes):
        pieces = [centred(patch_of(section, i).astype(f32)) for i in nodes]
        found = spectra([piece[0] for piece in pieces])
        for i, (real, imag) in zip(nodes, found):
            spec_re[i] = real
            spec_im[i] = imag
        return [piece[1] for piece in pieces]

    def checkers(section):
        return [total(patch_of(section, i).astype(f32) * tables[2]) for i in range(quarter_nodes)]

    up_ok = (sub_row > 0).astype(f32)
    down_ok = (sub_row < per_section - 1).astype(f32)
    left_ok = jnp.logical_and(lane > 0, lane < grid_cols).astype(f32)
    right_ok = (lane < grid_cols - 1).astype(f32)
    count = up_ok + down_ok + left_ok + right_ok

    def relax(flow, mask):
        weight = anchor_weight * mask
        pull = weight * flow
        scale = 1.0 / (weight + count)
        d = flow * mask
        for _ in range(SWEEPS):
            near = (
                up_ok * pltpu.roll(d, 1, 0)
                + down_ok * pltpu.roll(d, 2 * per_section - 1, 0)
                + left_ok * pltpu.roll(d, 1, 1)
                + right_ok * pltpu.roll(d, LANES - 1, 1)
            )
            d = (pull + near) * scale
        return jnp.where(lane < grid_cols, d, 0.0)

    corr_row = lax.broadcasted_iota(jnp.int32, (PADDED, PADDED), 0)
    corr_col = lax.broadcasted_iota(jnp.int32, (PADDED, PADDED), 1)
    inside = jnp.logical_and(corr_row < WINDOW, corr_col < WINDOW)

    def arrived(section, half):
        pltpu.make_async_copy(
            raw.at[section, half], raw.at[section, half], strip_recv.at[section, half]
        ).wait()

    def flows(section, previous, own_spread, nodes):
        pieces = [centred(patch) for patch in previous]
        found = spectra([piece[0] for piece in pieces])
        row_offset = offsets[0, section]
        col_offset = offsets[1, section]
        row_cos = window[0, pl.ds(row_offset + REACH, PADDED), :]
        row_sin = window[1, pl.ds(row_offset + REACH, PADDED), :]
        col_cos = split(window[0, pl.ds(col_offset + REACH, PADDED), :])
        col_sin = split(window[1, pl.ds(col_offset + REACH, PADDED), :])
        row_table = split(jnp.concatenate([row_cos, row_sin], axis=0))
        row_shift = (corr_row - HALF + row_offset).astype(f32)
        col_shift = (corr_col - HALF + col_offset).astype(f32)
        half_re, half_im = [], []
        for i, (prev_re, prev_im) in zip(nodes, found):
            own_re, own_im = spec_re[i], spec_im[i]
            cross_re = own_re * prev_re + own_im * prev_im
            cross_im = own_im * prev_re - own_re * prev_im
            part_re = mm3(row_table, split(cross_re))
            part_im = mm3(row_table, split(cross_im))
            half_re.append(part_re[:PADDED] - part_im[PADDED:])
            half_im.append(part_im[:PADDED] + part_re[PADDED:])
        correlation = mm3(
            split(jnp.concatenate(half_re, axis=0)), col_cos, mm_nt
        ) - mm3(split(jnp.concatenate(half_im, axis=0)), col_sin, mm_nt)
        tile = jnp.zeros(shape, f32)
        for k, i in enumerate(nodes):
            scale = sharpness / (float(PATCH) ** 4 * own_spread[k] * pieces[k][1])
            score = correlation[k * PADDED : (k + 1) * PADDED] * scale
            weights = jnp.where(inside, jnp.exp(score), 0.0)
            inverse = 1.0 / total(weights)
            flow_row = total(weights * row_shift) * inverse
            flow_col = total(weights * col_shift) * inverse
            here = lane == chain * quarter_nodes + i
            tile = jnp.where(jnp.logical_and(here, sub == row), flow_row, tile)
            tile = jnp.where(
                jnp.logical_and(here, sub == row + per_section), flow_col, tile
            )
        return tile

    def receive(index, away):
        def take(other):
            pltpu.make_async_copy(
                flow_slots.at[index, other], flow_slots.at[index, other], flow_recv.at[index, other]
            ).wait()
            return flow_slots[index, other]

        base = (chain + away) * per_section
        if away == 0:
            mine = lax.rem(me, per_section)
            found = flow_sum[index]
            for j in range(1, per_section):
                found = found + take(base + lax.rem(mine + j, per_section))
            flow_sum[index] = found
        else:

            @pl.when(jnp.logical_and(chain + away >= 0, chain + away < SECTIONS))
            def _():
                found = flow_sum[index]
                for j in range(per_section):
                    found = found + take(base + j)
                flow_sum[index] = found

    everyone = list(range(quarter_nodes))
    d = None
    for section in range(1, SECTIONS):
        index = section - 1
        if section == 1:
            tile = jnp.zeros(shape, f32)
            for half in range(HALVES):
                nodes = everyone[half * part_nodes : (half + 1) * part_nodes]
                arrived(1, half)
                arrived(0, half)
                spread = own_spectra(1, nodes)
                previous = [patch_of(0, i).astype(f32) for i in nodes]
                tile = tile + flows(1, previous, spread, nodes)
        else:
            pick_rows = jnp.sum(
                jnp.where(sub == row, d, 0.0), axis=0, keepdims=True
            )
            pick_cols = jnp.sum(
                jnp.where(sub == row + per_section, d, 0.0), axis=0, keepdims=True
            )
            terms = term_rows(pick_rows, pick_cols)
            term_lane = lax.broadcasted_iota(jnp.int32, terms.shape, 1)
            previous = []
            for i in everyone:
                wanted = term_lane == chain * quarter_nodes + i
                column = jnp.sum(jnp.where(wanted, terms, 0.0), axis=1, keepdims=True)
                moved = warp_patch(patch_of(index, i), column, corners[i], tables)
                previous.append(moved.astype(bf16).astype(f32))
            tile = flows(section, previous, spread, everyone)
        flow_tile[index] = tile
        flow_sum[index] = tile
        copies = []
        for step in range(1, tile_count):
            peer = lax.rem(me + step, tile_count)
            copy = pltpu.make_async_remote_copy(
                src_ref=flow_tile.at[index],
                dst_ref=flow_slots.at[index, me],
                send_sem=flow_send.at[index, step],
                recv_sem=flow_recv.at[index, me],
                device_id={"tile": peer},
                device_id_type=MESH,
            )
            copy.start()
            copies.append(copy)
        if section == 1:
            for copy in mask_copies:
                copy.wait()
        if section < SECTIONS - 1:
            for half in range(HALVES):
                arrived(section + 1, half)
            spread = own_spectra(section + 1, everyone)
            corners = checkers(section)
            mask = jnp.zeros(shape, f32)
            for r in range(per_section):
                mask = mask + mask_slots[(section * per_section + r + lead) % tile_count]
            for away in range(-reach, reach + 1):
                receive(index, away)
            d = relax(flow_sum[index], mask)
        sends += copies
    mask = jnp.zeros(shape, f32)
    for r in range(per_section):
        mask = mask + mask_slots[
            lax.rem(group * per_section + r + lead, tile_count)
        ]
    for copy in sends:
        copy.wait_send()
    for index in range(SECTIONS - 1):
        for away in range(1 - SECTIONS, SECTIONS):
            if abs(away) > reach or index == SECTIONS - 2:
                receive(index, away)
    flow = jnp.zeros(shape, f32)
    for index in range(SECTIONS - 1):
        flow = jnp.where(group == index + 1, flow_sum[index], flow)
    home = jnp.where(group == 0, 0.0, relax(flow, mask))
    out_row = jnp.sum(jnp.where(sub == row, home, 0.0), axis=0, keepdims=True)
    out_col = jnp.sum(jnp.where(sub == row + per_section, home, 0.0), axis=0, keepdims=True)
    out_ref[...] = jnp.concatenate([out_row, out_col], axis=0)


def warp_kernel(shift_ref, strip_in, tables_in, out, node_ref, strip, warp_tables, result, sems):
    pieces = strip.shape[0]
    width = strip.shape[2]
    table_load = pltpu.make_async_copy(tables_in, warp_tables, sems.at[2 * pieces])
    table_load.start()
    loads, stores = [], []
    for k in range(pieces):
        where = pl.ds(k * width, width)
        loads.append(pltpu.make_async_copy(strip_in.at[:, where], strip.at[k], sems.at[k]))
        stores.append(
            pltpu.make_async_copy(result.at[k], out.at[:, where], sems.at[pieces + k])
        )
        loads[k].start()
    terms = term_rows(shift_ref[0:1, :], shift_ref[1:2, :])
    lane = lax.broadcasted_iota(jnp.int32, terms.shape, 1)
    nodes = node_ref.shape[2]
    node_ref[0] = shift_ref[0:1, 0:nodes]
    node_ref[1] = shift_ref[1:2, 0:nodes]
    table_load.wait()
    tables = [warp_tables[i] for i in range(4)]
    for k in range(pieces):
        loads[k].wait()
        for j, s in enumerate(patch_slices(width)):
            i = k * (width // PATCH) + j
            column = jnp.sum(jnp.where(lane == i, terms, 0.0), axis=1, keepdims=True)
            patch = strip[k, :, s]
            checker = total(patch.astype(f32) * tables[2])
            result[k, :, s] = warp_patch(patch, column, checker, tables).astype(bf16)
        stores[k].start()
    for copy in stores:
        copy.wait()


def shards(tile_count, sections, valid_mask, coarse_offsets):
    per_section = tile_count // SECTIONS
    grid_cols = valid_mask.shape[1]
    quarter = sections.shape[1] // SECTIONS
    nodes = quarter // PATCH
    steps = SECTIONS - 1
    tile_shape = (2 * per_section, LANES)
    vmem = pl.BlockSpec(memory_space=pltpu.VMEM)
    tables = constants()
    hbm = pl.BlockSpec(memory_space=pltpu.HBM)
    shift = pl.pallas_call(
        functools.partial(chain_kernel, tile_count, grid_cols),
        out_shape=jax.ShapeDtypeStruct((2, LANES), f32),
        in_specs=[hbm] * (CONSTANTS + 3),
        out_specs=vmem,
        scratch_shapes=[pltpu.VMEM(table.shape, table.dtype) for table in tables]
        + [
            pltpu.SMEM(coarse_offsets.shape[::-1], jnp.int32),
            pltpu.VMEM(valid_mask.shape, jnp.int32),
            pltpu.SemaphoreType.DMA((CONSTANTS + 2,)),
            pltpu.VMEM((SECTIONS, HALVES, PATCH, quarter // HALVES), bf16),
            pltpu.VMEM(tile_shape, f32),
            pltpu.VMEM((tile_count,) + tile_shape, f32),
            pltpu.VMEM((steps,) + tile_shape, f32),
            pltpu.VMEM((steps, tile_count) + tile_shape, f32),
            pltpu.VMEM((steps,) + tile_shape, f32),
            pltpu.VMEM((nodes, PATCH, PATCH), f32),
            pltpu.VMEM((nodes, PATCH, PATCH), f32),
            pltpu.SemaphoreType.DMA((SECTIONS, HALVES)),
            pltpu.SemaphoreType.DMA((SECTIONS, HALVES)),
            pltpu.SemaphoreType.DMA((tile_count,)),
            pltpu.SemaphoreType.DMA((tile_count,)),
            pltpu.SemaphoreType.DMA((steps, tile_count)),
            pltpu.SemaphoreType.DMA((steps, tile_count)),
        ],
        compiler_params=pltpu.CompilerParams(
            collective_id=0, has_side_effects=True
        ),
        name="chain",
    )(coarse_offsets.T, valid_mask, *tables, sections)
    return pl.pallas_call(
        warp_kernel,
        out_shape=(
            jax.ShapeDtypeStruct(sections.shape, bf16),
            jax.ShapeDtypeStruct((2, 1, grid_cols), f32),
        ),
        in_specs=[vmem, hbm, hbm],
        out_specs=(hbm, vmem),
        scratch_shapes=[
            pltpu.VMEM((PIECES, PATCH, sections.shape[1] // PIECES), bf16),
            pltpu.VMEM(tables[-1].shape, f32),
            pltpu.VMEM((PIECES, PATCH, sections.shape[1] // PIECES), bf16),
            pltpu.SemaphoreType.DMA((2 * PIECES + 1,)),
        ],
        name="warp",
    )(shift, sections, tables[-1])


def solution(mesh):
    placed = (P(("parts", "tile"), None), P(("parts", "tile"), None), P("parts", None))
    return jax.shard_map(
        functools.partial(shards, mesh.shape["tile"]),
        mesh=mesh,
        in_specs=placed,
        out_specs=(P(("parts", "tile"), None), P(None, ("parts", "tile"), None)),
        check_vma=False,
    )
```

```python
import functools

import jax
import jax.numpy as jnp
import numpy as np
from jax import lax
from jax.experimental import pallas as pl
from jax.experimental.pallas import tpu as pltpu
from jax.sharding import PartitionSpec as P

SECTIONS = 4
PATCH = 128
HALF = 4
SWEEPS = 3
REACH = 3
WINDOW = 2 * HALF + 1
PADDED = 16
LANES = 128
CONSTANTS = 6
HALVES = 2
PIECES = 2

sharpness = 12.0
anchor_weight = 2.0
MESH = pl.DeviceIdType.MESH
f32 = jnp.float32
bf16 = jnp.bfloat16


def split(value):
    high = value.astype(bf16)
    return high, (value - high.astype(f32)).astype(bf16)


def mm(a, b):
    return jnp.dot(a, b, preferred_element_type=f32)


def mm_nt(a, b):
    return lax.dot_general(a, b, (((1,), (1,)), ((), ())), preferred_element_type=f32)


def mm3(a, b, product=mm):
    return product(a[0], b[0]) + (product(a[0], b[1]) + product(a[1], b[0]))


def constants():
    n = PATCH
    k = np.arange(n)
    angle = 2 * np.pi * ((k[:, None] * k[None, :]) % n) / n
    stacked = np.concatenate([np.cos(angle), np.sin(angle)], axis=0)
    dft_hi = np.asarray(stacked, bf16)
    dft_t_hi = np.asarray(stacked.T, bf16)
    dft_lo = np.asarray(stacked - dft_hi.astype(np.float64), bf16)
    dft_hi2 = np.concatenate([dft_hi, dft_lo], axis=0)
    dft_t_hi2 = np.concatenate([dft_t_hi, np.asarray(stacked.T - dft_t_hi.astype(np.float64), bf16)], axis=1)
    u = np.arange(-HALF - REACH, -HALF - REACH + 24)
    window_angle = 2 * np.pi * ((u[:, None] * k[None, :]) % n) / n
    exact = np.cos(angle)
    gain = (dft_hi[:n].astype(np.float64) * exact).sum(axis=1) / (exact * exact).sum(axis=1)
    window = np.stack([np.cos(window_angle), np.sin(window_angle)])
    window = window.astype(np.float32)
    half_angle = np.pi * k / n
    sign = 1.0 - 2.0 * (k % 2)
    warp = np.zeros((8, n), np.float32)
    warp[:4] = np.stack([np.sin(half_angle), np.cos(half_angle), sign, k])
    parity = (sign[:, None] * sign[None, :]).astype(np.float32)
    sums = (dft_hi.astype(np.float64)+dft_lo.astype(np.float64)).sum(axis=1, keepdims=True)
    sums = np.broadcast_to(sums, (2 * n, n)).astype(np.float32)
    return dft_hi2, dft_t_hi2, sums, window, warp, parity


def shift_terms(d):
    whole = jnp.round(d)
    frac = d - whole
    odd = jnp.abs(whole - 2.0 * jnp.round(whole * 0.5))
    sine = jnp.sin(jnp.pi * frac)
    signed = jnp.where(odd > 0.5, -sine, sine) * (1.0 / PATCH)
    angle = d * (np.pi / PATCH)
    tangent = jnp.sin(angle) / jnp.cos(angle)
    small = frac * (np.pi / PATCH)
    tiny = jnp.abs(frac) < 1e-6
    peak = jnp.where(
        tiny, 1.0, sine * jnp.cos(small) / jnp.where(tiny, 1.0, PATCH * jnp.sin(small))
    )
    return tangent, signed, peak, whole


def kernel_rows(terms, tables):
    columns = jnp.transpose(terms)[:LANES]
    sine, cosine, parity, gap = [tables[i : i + 1, :] for i in range(4)]
    found = []
    for base, forward in ((0, False), (4, True)):
        tangent, signed, peak, whole = [columns[:, base + i : base + i + 1] for i in range(4)]
        if forward:
            bottom = cosine * tangent + sine
            top = cosine - sine * tangent
            centre = jnp.where(whole > 0, PATCH - whole, -whole)
        else:
            bottom = cosine * tangent - sine
            top = cosine + sine * tangent
            centre = jnp.where(whole < 0, whole + PATCH, whole)
        found.append(jnp.where(gap == centre, peak, (signed * parity) * (top / bottom)))
    corner = columns[:, 1:2] * columns[:, 5:6]
    return found[0], found[1], corner


def circulant(row):
    spread = jnp.broadcast_to(row, (PATCH, PATCH))
    return split(pltpu.roll(spread, 0, 1, stride=1, stride_axis=0))


def warp_patch(patch, rows, i, checker, parity):
    left = circulant(rows[0][i : i + 1, :])
    right = circulant(rows[1][i : i + 1, :])
    both = mm(patch, jnp.concatenate(right, axis=1))
    high, low = split(both[:, :PATCH] + both[:, PATCH:])
    lower = jnp.concatenate([high, jnp.zeros_like(low)], axis=1)
    inner = jnp.concatenate([jnp.concatenate([high, low], axis=1), lower], axis=0)
    moved = mm(jnp.concatenate(left, axis=1), inner)
    corner = (rows[2][i : i + 1, :] * checker) * parity
    return (moved[:, :PATCH] + moved[:, PATCH:]) - corner


def total(value):
    return jnp.sum(jnp.sum(value, axis=0, keepdims=True), axis=1, keepdims=True)


def term_rows(d_rows, d_cols):
    both = jnp.concatenate([d_rows, d_cols], axis=0)
    tangent, signed, peak, whole = shift_terms(both)
    pieces = [t[i : i + 1] for i in range(2) for t in (tangent, signed, peak, whole)]
    return jnp.concatenate(pieces, axis=0)


def centred(patch):
    mean_level = total(patch) * (1.0 / (PATCH * PATCH))
    centre = patch - mean_level
    variance = total(centre * centre) * (1.0 / (PATCH * PATCH))
    return mean_level, jnp.sqrt(variance + 1e-05)


def patch_slices(width):
    return [slice(i * PATCH, (i + 1) * PATCH) for i in range(width // PATCH)]


def chain_kernel(
    tile_count,
    grid_cols,
    offsets_in,
    mask_in,
    *rest,
):
    constant_in = rest[:CONSTANTS]
    constant_ref = rest[CONSTANTS + 2 : 2 * CONSTANTS + 2]
    dft_ref, dft_t_ref, sums_ref, window, warp_tables, parity_ref = constant_ref
    strip, out_ref = rest[CONSTANTS : CONSTANTS + 2]
    (
    offsets,
    mask_ref,
    load_sem,
    raw,
    mask_tile,
    mask_slots,
    flow_tile,
    flow_slots,
    flow_sum,
    spec_re,
    spec_im,
    strip_send,
    strip_recv,
    mask_send,
    mask_recv,
    flow_send,
    flow_recv,
    ) = rest[2 * CONSTANTS + 2 :]
    per_section = tile_count // SECTIONS
    me = lax.axis_index("tile")
    lead = per_section // 2
    rotated = lax.rem(me + tile_count - lead, tile_count)
    group = rotated // per_section
    row = lax.rem(rotated, per_section)
    chain = me // per_section
    quarter = raw.shape[3] * HALVES
    part = raw.shape[3]
    quarter_nodes = quarter // PATCH
    part_nodes = part // PATCH
    reach = -(-SWEEPS // quarter_nodes)

    barrier = pltpu.get_barrier_semaphore()
    for step in range(1, tile_count):
        peer = lax.rem(me + step, tile_count)
        pl.semaphore_signal(barrier, inc=1, device_id={"tile": peer}, device_id_type=MESH)

    loads = [
        pltpu.make_async_copy(source, target, load_sem.at[i])
        for i, (source, target) in enumerate(
            zip((mask_in, offsets_in) + constant_in, (mask_ref, offsets) + constant_ref)
        )
    ]
    for copy in loads:
        copy.start()
    def columns(owner, half):
        return strip.at[:, pl.ds(pl.multiple_of(owner * quarter + half * part, LANES), part)]

    for half in range(HALVES):
        pltpu.make_async_copy(
            columns(chain, half), raw.at[group, half], strip_recv.at[group, half]
        ).start()
    loads[0].wait()
    shape = (2 * per_section, LANES)
    sub = lax.broadcasted_iota(jnp.int32, shape, 0)
    lane = lax.broadcasted_iota(jnp.int32, shape, 1)
    sub_row = lax.rem(sub, per_section)
    mask_tile[...] = jnp.zeros(shape, f32)
    mask_tile[0:1, 0:grid_cols] = mask_ref[...].astype(f32)
    mask_row = mask_tile[0:1, :]
    mask_tile[...] = jnp.where(sub_row == row, mask_row, 0.0)
    mask_slots[me] = mask_tile[...]

    pl.semaphore_wait(barrier, tile_count - 1)

    mask_copies = []
    for step in range(1, tile_count):
        peer = lax.rem(me + step, tile_count)
        copy = pltpu.make_async_remote_copy(
            src_ref=mask_tile,
            dst_ref=mask_slots.at[me],
            send_sem=mask_send.at[step],
            recv_sem=mask_recv.at[step],
            device_id={"tile": peer},
            device_id_type=MESH,
        )
        copy.start()
        mask_copies.append(copy)

    sends = []
    for half in range(HALVES):
        for step in range(1, SECTIONS):
            copy = pltpu.make_async_remote_copy(
                src_ref=columns(lax.rem(chain + step, SECTIONS), half),
                dst_ref=raw.at[group, half],
                send_sem=strip_send.at[step, half],
                recv_sem=strip_recv.at[group, half],
                device_id={"tile": lax.rem(me + step * per_section, tile_count)},
                device_id_type=MESH,
            )
            copy.start()
            sends.append(copy)
    for copy in loads[1:]:
        copy.wait()
    tables = warp_tables[...]
    parity = parity_ref[...]
    dft = dft_ref[...]
    dft_t = dft_t_ref[...]
    sums = sums_ref[...]

    def spectra(patches, levels):
        found = []
        for patch, level in zip(patches, levels):
            first = mm(dft, patch)
            first = (first[: 2 * PATCH] + first[2 * PATCH :] - sums * level).astype(bf16)
            both = mm(first, dft_t)
            both = both[:, : 2 * PATCH] + both[:, 2 * PATCH :]
            real = both[:PATCH, :PATCH] - both[PATCH:, PATCH:]
            imag = -(both[:PATCH, PATCH:] + both[PATCH:, :PATCH])
            found.append((real, imag))
        return found

    def patch_of(section, i):
        start = (i % part_nodes) * PATCH
        return raw[section, i // part_nodes, :, start : start + PATCH]

    def own_spectra(section, nodes):
        patches = [patch_of(section, i) for i in nodes]
        pieces = [centred(patch.astype(f32)) for patch in patches]
        found = spectra(patches, [piece[0] for piece in pieces])
        for i, (real, imag) in zip(nodes, found):
            spec_re[i] = real
            spec_im[i] = imag
        return [piece[1] for piece in pieces]

    def checkers(section):
        return [total(patch_of(section, i).astype(f32) * parity) for i in range(quarter_nodes)]

    up_ok = (sub_row > 0).astype(f32)
    down_ok = (sub_row < per_section - 1).astype(f32)
    left_ok = jnp.logical_and(lane > 0, lane < grid_cols).astype(f32)
    right_ok = (lane < grid_cols - 1).astype(f32)
    count = up_ok + down_ok + left_ok + right_ok

    def relax(flow, mask):
        weight = anchor_weight * mask
        pull = weight * flow
        scale = 1.0 / (weight + count)
        d = flow * mask
        for _ in range(SWEEPS):
            near = (
                up_ok * pltpu.roll(d, 1, 0)
                + down_ok * pltpu.roll(d, 2 * per_section - 1, 0)
                + left_ok * pltpu.roll(d, 1, 1)
                + right_ok * pltpu.roll(d, LANES - 1, 1)
            )
            d = (pull + near) * scale
        return jnp.where(lane < grid_cols, d, 0.0)

    corr_row = lax.broadcasted_iota(jnp.int32, (PADDED, PADDED), 0)
    corr_col = lax.broadcasted_iota(jnp.int32, (PADDED, PADDED), 1)
    inside = jnp.logical_and(corr_row < WINDOW, corr_col < WINDOW)

    def arrived(section, half):
        pltpu.make_async_copy(
            raw.at[section, half], raw.at[section, half], strip_recv.at[section, half]
        ).wait()

    def flows(section, previous, own_spread, nodes):
        pieces = [centred(patch.astype(f32)) for patch in previous]
        found = spectra(previous, [piece[0] for piece in pieces])
        row_offset = offsets[0, section]
        col_offset = offsets[1, section]
        row_cos = window[0, pl.ds(row_offset + REACH, PADDED), :]
        row_sin = window[1, pl.ds(row_offset + REACH, PADDED), :]
        col_cos = split(window[0, pl.ds(col_offset + REACH, PADDED), :])
        col_sin = split(window[1, pl.ds(col_offset + REACH, PADDED), :])
        row_table = jnp.concatenate(split(jnp.concatenate([row_cos, row_sin], axis=0)), axis=0)
        row_shift = (corr_row - HALF + row_offset).astype(f32)
        col_shift = (corr_col - HALF + col_offset).astype(f32)
        half_re, half_im = [], []
        for i, (prev_re, prev_im) in zip(nodes, found):
            own_re, own_im = spec_re[i], spec_im[i]
            cross_re = own_re * prev_re + own_im * prev_im
            cross_im = own_im * prev_re - own_re * prev_im
            cross = jnp.concatenate([cross_re, cross_im], axis=1).astype(bf16)
            parts = mm(row_table, cross)
            parts = parts[: 2 * PADDED] + parts[2 * PADDED :]
            part_re = parts[:, :PATCH]
            part_im = parts[:, PATCH:]
            half_re.append(part_re[:PADDED] - part_im[PADDED:])
            half_im.append(part_im[:PADDED] + part_re[PADDED:])
        correlation = mm3(
            split(jnp.concatenate(half_re, axis=0)), col_cos, mm_nt
        ) - mm3(split(jnp.concatenate(half_im, axis=0)), col_sin, mm_nt)
        tile = jnp.zeros(shape, f32)
        for k, i in enumerate(nodes):
            scale = sharpness / (float(PATCH) ** 4 * own_spread[k] * pieces[k][1])
            score = correlation[k * PADDED : (k + 1) * PADDED] * scale
            weights = jnp.where(inside, jnp.exp(score), 0.0)
            inverse = 1.0 / total(weights)
            flow_row = total(weights * row_shift) * inverse
            flow_col = total(weights * col_shift) * inverse
            here = lane == chain * quarter_nodes + i
            tile = jnp.where(jnp.logical_and(here, sub == row), flow_row, tile)
            tile = jnp.where(
                jnp.logical_and(here, sub == row + per_section), flow_col, tile
            )
        return tile

    def receive(index, away):
        def take(other):
            pltpu.make_async_copy(
                flow_slots.at[index, other], flow_slots.at[index, other], flow_recv.at[index, other]
            ).wait()
            return flow_slots[index, other]

        base = (chain + away) * per_section
        if away == 0:
            mine = lax.rem(me, per_section)
            found = flow_sum[index]
            for j in range(1, per_section):
                found = found + take(base + lax.rem(mine + j, per_section))
            flow_sum[index] = found
        else:

            @pl.when(jnp.logical_and(chain + away >= 0, chain + away < SECTIONS))
            def _():
                found = flow_sum[index]
                for j in range(per_section):
                    found = found + take(base + j)
                flow_sum[index] = found

    everyone = list(range(quarter_nodes))
    d = None
    for section in range(1, SECTIONS):
        index = section - 1
        if section == 1:
            tile = jnp.zeros(shape, f32)
            for half in range(HALVES):
                nodes = everyone[half * part_nodes : (half + 1) * part_nodes]
                arrived(1, half)
                arrived(0, half)
                spread = own_spectra(1, nodes)
                previous = [patch_of(0, i) for i in nodes]
                tile = tile + flows(1, previous, spread, nodes)
        else:
            pick_rows = jnp.sum(
                jnp.where(sub == row, d, 0.0), axis=0, keepdims=True
            )
            pick_cols = jnp.sum(
                jnp.where(sub == row + per_section, d, 0.0), axis=0, keepdims=True
            )
            terms = term_rows(pick_rows, pick_cols)
            term_lane = lax.broadcasted_iota(jnp.int32, terms.shape, 1)
            placed = jnp.zeros(terms.shape, f32)
            for i in everyone:
                wanted = term_lane == chain * quarter_nodes + i
                column = jnp.sum(jnp.where(wanted, terms, 0.0), axis=1, keepdims=True)
                placed = jnp.where(term_lane == i, column, placed)
            rows = kernel_rows(placed, tables)
            previous = [
                warp_patch(patch_of(index, i), rows, i, corners[i], parity).astype(bf16)
                for i in everyone
            ]
            tile = flows(section, previous, spread, everyone)
        flow_tile[index] = tile
        flow_sum[index] = tile
        copies = []
        for step in range(1, tile_count):
            peer = lax.rem(me + step, tile_count)
            copy = pltpu.make_async_remote_copy(
                src_ref=flow_tile.at[index],
                dst_ref=flow_slots.at[index, me],
                send_sem=flow_send.at[index, step],
                recv_sem=flow_recv.at[index, me],
                device_id={"tile": peer},
                device_id_type=MESH,
            )
            copy.start()
            copies.append(copy)
        if section == 1:
            for copy in mask_copies:
                copy.wait()
        if section < SECTIONS - 1:
            for half in range(HALVES):
                arrived(section + 1, half)
            spread = own_spectra(section + 1, everyone)
            corners = checkers(section)
            mask = jnp.zeros(shape, f32)
            for r in range(per_section):
                mask = mask + mask_slots[(section * per_section + r + lead) % tile_count]
            for away in range(-reach, reach + 1):
                receive(index, away)
            d = relax(flow_sum[index], mask)
        sends += copies
    mask = jnp.zeros(shape, f32)
    for r in range(per_section):
        mask = mask + mask_slots[
            lax.rem(group * per_section + r + lead, tile_count)
        ]
    for copy in sends:
        copy.wait_send()
    for index in range(SECTIONS - 1):
        for away in range(1 - SECTIONS, SECTIONS):
            if abs(away) > reach or index == SECTIONS - 2:
                receive(index, away)
    flow = jnp.zeros(shape, f32)
    for index in range(SECTIONS - 1):
        flow = jnp.where(group == index + 1, flow_sum[index], flow)
    home = jnp.where(group == 0, 0.0, relax(flow, mask))
    out_row = jnp.sum(jnp.where(sub == row, home, 0.0), axis=0, keepdims=True)
    out_col = jnp.sum(jnp.where(sub == row + per_section, home, 0.0), axis=0, keepdims=True)
    out_ref[...] = jnp.concatenate([out_row, out_col], axis=0)


def warp_kernel(
    shift_ref, strip_in, warp_tables, parity_ref, out, node_ref, strip, result, sems
):
    pieces = strip.shape[0]
    width = strip.shape[2]
    loads, stores = [], []
    for k in range(pieces):
        where = pl.ds(k * width, width)
        loads.append(pltpu.make_async_copy(strip_in.at[:, where], strip.at[k], sems.at[k]))
        stores.append(
            pltpu.make_async_copy(result.at[k], out.at[:, where], sems.at[pieces + k])
        )
        loads[k].start()
    nodes = node_ref.shape[2]
    node_ref[0] = shift_ref[0:1, 0:nodes]
    node_ref[1] = shift_ref[1:2, 0:nodes]
    rows = kernel_rows(term_rows(shift_ref[0:1, :], shift_ref[1:2, :]), warp_tables[...])
    parity = parity_ref[...]
    for k in range(pieces):
        loads[k].wait()
        for j, s in enumerate(patch_slices(width)):
            i = k * (width // PATCH) + j
            patch = strip[k, :, s]
            checker = total(patch.astype(f32) * parity)
            result[k, :, s] = warp_patch(patch, rows, i, checker, parity).astype(bf16)
        stores[k].start()
    for copy in stores:
        copy.wait()


def shards(tile_count, sections, valid_mask, coarse_offsets):
    per_section = tile_count // SECTIONS
    grid_cols = valid_mask.shape[1]
    quarter = sections.shape[1] // SECTIONS
    nodes = quarter // PATCH
    steps = SECTIONS - 1
    tile_shape = (2 * per_section, LANES)
    vmem = pl.BlockSpec(memory_space=pltpu.VMEM)
    tables = constants()
    hbm = pl.BlockSpec(memory_space=pltpu.HBM)
    shift = pl.pallas_call(
        functools.partial(chain_kernel, tile_count, grid_cols),
        out_shape=jax.ShapeDtypeStruct((2, LANES), f32),
        in_specs=[hbm] * (CONSTANTS + 3),
        out_specs=vmem,
        scratch_shapes=[pltpu.VMEM(table.shape, table.dtype) for table in tables]
        + [
            pltpu.SMEM(coarse_offsets.shape[::-1], jnp.int32),
            pltpu.VMEM(valid_mask.shape, jnp.int32),
            pltpu.SemaphoreType.DMA((CONSTANTS + 2,)),
            pltpu.VMEM((SECTIONS, HALVES, PATCH, quarter // HALVES), bf16),
            pltpu.VMEM(tile_shape, f32),
            pltpu.VMEM((tile_count,) + tile_shape, f32),
            pltpu.VMEM((steps,) + tile_shape, f32),
            pltpu.VMEM((steps, tile_count) + tile_shape, f32),
            pltpu.VMEM((steps,) + tile_shape, f32),
            pltpu.VMEM((nodes, PATCH, PATCH), f32),
            pltpu.VMEM((nodes, PATCH, PATCH), f32),
            pltpu.SemaphoreType.DMA((SECTIONS, HALVES)),
            pltpu.SemaphoreType.DMA((SECTIONS, HALVES)),
            pltpu.SemaphoreType.DMA((tile_count,)),
            pltpu.SemaphoreType.DMA((tile_count,)),
            pltpu.SemaphoreType.DMA((steps, tile_count)),
            pltpu.SemaphoreType.DMA((steps, tile_count)),
        ],
        compiler_params=pltpu.CompilerParams(
            collective_id=0, has_side_effects=True
        ),
        name="chain",
    )(coarse_offsets.T, valid_mask, *tables, sections)
    return pl.pallas_call(
        warp_kernel,
        out_shape=(
            jax.ShapeDtypeStruct(sections.shape, bf16),
            jax.ShapeDtypeStruct((2, 1, grid_cols), f32),
        ),
        in_specs=[vmem, hbm, vmem, vmem],
        out_specs=(hbm, vmem),
        scratch_shapes=[
            pltpu.VMEM((PIECES, PATCH, sections.shape[1] // PIECES), bf16),
            pltpu.VMEM((PIECES, PATCH, sections.shape[1] // PIECES), bf16),
            pltpu.SemaphoreType.DMA((2 * PIECES,)),
        ],
        name="warp",
    )(shift, sections, tables[-2], tables[-1])


def solution(mesh):
    placed = (P(("parts", "tile"), None), P(("parts", "tile"), None), P("parts", None))
    return jax.shard_map(
        functools.partial(shards, mesh.shape["tile"]),
        mesh=mesh,
        in_specs=placed,
        out_specs=(P(("parts", "tile"), None), P(None, ("parts", "tile"), None)),
        check_vma=False,
    )
```
